256 devices in a mesh: dp: 16 (over x, y_lo, core), feat: 16 (over z, y_hi).
Axes of the slice: x: 4, y: 4 (y_hi: 2, y_lo: 2; y = y_hi * 2 + y_lo), z: 8, core: 2. Of those that a mesh axis runs over, the one named last changes fastest.
Arguments:
- tokens: bfloat16 [16384, 16384], P('dp', 'feat'), may hold values from -6 to 6
- cotangent: bfloat16 [16384, 16384], P('dp', 'feat'), may hold values from -6 to 6
- first_right: bfloat16 [128, 128, 128], P('feat'), may hold values from -0.5 to 0.5
- first_left: bfloat16 [128, 128, 512], P('feat'), may hold values from -0.5 to 0.5
- second_right: bfloat16 [128, 512, 128], P('feat'), may hold values from -0.25 to 0.25
- second_left: bfloat16 [128, 128, 128], P('feat'), may hold values from -0.5 to 0.5
Outputs:
- output: bfloat16 [16384, 16384], P('dp', 'feat')
- token_grad: bfloat16 [16384, 16384], P('dp', 'feat')
- first_right_grad: float32 [128, 128, 128], P('dp', 'feat')
- first_left_grad: float32 [128, 128, 512], P('dp', 'feat')
- second_right_grad: float32 [512, 128, 128], P('dp', 'feat')
- second_left_grad: float32 [128, 128, 128], P('dp', 'feat')
The draws below stay inside these ranges and needn't reach their ends.
All inputs are finite; a program needn't handle non-finite values.
Results may differ from the reference program's by a relative error of at most 0.0064.
Values may be sent and summed in bfloat16 or wider, within the bound.
No kernel may reach another device: no remote copies, remote signals or barrier semaphores. Data moves between devices by JAX's collectives and lax.ppermute only.
A program may use at most 128 MiB of HBM per device.

```python
import jax
import jax.numpy as jnp
from jax import lax

NB = 128
BS = 128
HB = 512
D = 16384
TOK_DEV = 1024
TOKENS = 16384


def block_levels(key, extent, cuts, smallest, high):
    gain = 1.0
    for axis_at, shards_of in cuts:
        draws = jax.random.uniform(jax.random.fold_in(jax.random.fold_in(key, 6), axis_at), (shards_of,), jnp.float32, smallest / len(cuts), high / len(cuts))
        gain = gain * jnp.repeat(jnp.exp(draws), extent[axis_at] // shards_of).reshape((-1,) + (1,) * (len(extent) - 1 - axis_at))
    return gain


def noise(rng, shape, scale, bound, pieces=(), held_as=jnp.bfloat16):
    factor_of = block_levels(rng, shape, pieces, -0.22, 0.18) if pieces else 1.0
    entries = jax.random.normal(rng, shape, jnp.float32) * scale * factor_of
    return jnp.minimum(jnp.maximum(entries, -bound), bound).astype(held_as)


def setup_inputs(seed: int = 0) -> dict:
    key_list = jax.random.split(jax.random.key(seed), 7)
    return {
        "tokens": noise(key_list[0], (TOKENS, D), 1.0, 6.0, ((0, 16), (1, 16))),
        "cotangent": noise(key_list[1], (TOKENS, D), 1.0, 6.0, ((0, 16), (1, 16))),
        "first_right": noise(key_list[2], (NB, BS, BS), BS ** -0.5, 0.5, ((0, 16),)),
        "first_left": noise(key_list[3], (BS, NB, HB), NB ** -0.5, 0.5, ((0, 16),)),
        "second_right": noise(key_list[4], (BS, HB, NB), HB ** -0.5, 0.25, ((0, 16),)),
        "second_left": noise(key_list[5], (NB, BS, BS), BS ** -0.5, 0.5, ((0, 16),)),
    }


def activate(value):
    return jax.nn.gelu(value, approximate=True)

def activate_grad(pre, upstream):
    _, pullback = jax.vjp(activate, pre)
    return pullback(upstream)[0]

def one_group(totals, pair, first_right, first_left, second_right, second_left):
    tok_rows, cot_rows = pair
    count_rows = tok_rows.shape[0]
    tok_blocks = tok_rows.reshape(count_rows, NB, BS).astype(jnp.float32)
    cot_blocks = cot_rows.reshape(count_rows, NB, BS).astype(jnp.float32)
    right_one = first_right.astype(jnp.float32)
    left_one = first_left.astype(jnp.float32)
    right_two = second_right.astype(jnp.float32)
    left_two = second_left.astype(jnp.float32)
    mixed = jnp.einsum('tij,ijk->tik', tok_blocks, right_one).astype(jnp.bfloat16)
    pre = jnp.einsum('tik,kih->tkh', mixed.astype(jnp.float32), left_one)
    hidden_act = activate(pre).astype(jnp.bfloat16)
    narrowed = jnp.einsum('tkh,khi->tki', hidden_act.astype(jnp.float32), right_two).astype(jnp.bfloat16)
    branch_out = jnp.einsum('tki,ikl->til', narrowed.astype(jnp.float32), left_two)
    output = (tok_blocks + branch_out).astype(jnp.bfloat16).reshape(count_rows, D)
    grad_narrow = jnp.einsum('til,ikl->tki', cot_blocks, left_two).astype(jnp.bfloat16)
    grad_act = jnp.einsum('tki,khi->tkh', grad_narrow.astype(jnp.float32), right_two)
    grad_pre = activate_grad(pre, grad_act).astype(jnp.bfloat16)
    grad_mixed = jnp.einsum('tkh,kih->tik', grad_pre.astype(jnp.float32), left_one).astype(jnp.bfloat16)
    token_grad = (cot_blocks + jnp.einsum('tik,ijk->tij', grad_mixed.astype(jnp.float32), right_one)).astype(jnp.bfloat16).reshape(count_rows, D)
    sl_term = jnp.einsum('tki,til->kil', narrowed.astype(jnp.float32), cot_blocks)
    sr_term = jnp.einsum('tkh,tki->hki', hidden_act.astype(jnp.float32), grad_narrow.astype(jnp.float32))
    fl_term = jnp.einsum('tik,tkh->ikh', mixed.astype(jnp.float32), grad_pre.astype(jnp.float32))
    fr_term = jnp.einsum('tij,tik->jik', tok_blocks, grad_mixed.astype(jnp.float32))
    new_totals = (totals[0] + fr_term, totals[1] + fl_term, totals[2] + sr_term, totals[3] + sl_term)
    return (new_totals, (output, token_grad))

def reference(tokens, cotangent, first_right, first_left, second_right, second_left):
    tok_groups = tokens.reshape(-1, TOK_DEV, D)
    cot_groups = cotangent.reshape(-1, TOK_DEV, D)
    start_totals = (jnp.zeros((BS, NB, BS), jnp.float32), jnp.zeros((NB, BS, HB), jnp.float32), jnp.zeros((HB, BS, NB), jnp.float32), jnp.zeros((BS, NB, BS), jnp.float32))

    def stepper(totals, pair):
        return one_group(totals, pair, first_right, first_left, second_right, second_left)
    totals, (outputs, grads_in) = lax.scan(stepper, start_totals, (tok_groups, cot_groups))
    return (outputs.reshape(TOKENS, D), grads_in.reshape(TOKENS, D), totals[0], totals[1], totals[2], totals[3])
```

```python
import jax
import jax.numpy as jnp
from jax import lax
from jax.sharding import PartitionSpec as P

BF = jnp.bfloat16
F32 = jnp.float32


def activate(value):
    return jax.nn.gelu(value, approximate=True)


def activate_grad(pre, upstream):
    _, pullback = jax.vjp(activate, pre)
    return pullback(upstream)[0]


def swap(blocks):
    return lax.all_to_all(blocks, "feat", split_axis=0, concat_axis=0, tiled=True)


def reduce_dp(term):
    me = lax.axis_index("dp")
    core, low, col = me & 1, (me >> 1) & 1, me >> 2
    rest = term.shape[1:]
    parts = term.reshape((4, 2, 2, term.shape[0] // 16) + rest)

    def pick(a, at, axis):
        starts = [at if n == axis else 0 for n in range(a.ndim)]
        sizes = [1 if n == axis else a.shape[n] for n in range(a.ndim)]
        one = lax.dynamic_slice(a, starts, sizes, allow_negative_indices=False)
        return lax.squeeze(one, (axis,))

    got = lax.ppermute(pick(parts, 1 - core, 2).astype(BF), "dp", [(d, d ^ 1) for d in range(16)])
    parts = pick(parts, core, 2) + got.astype(F32)
    got = lax.ppermute(pick(parts, 1 - low, 1).astype(BF), "dp", [(d, d ^ 2) for d in range(16)])
    parts = pick(parts, low, 1) + got.astype(F32)
    total = pick(parts, col, 0)
    for step in (1, 2, 3):
        got = lax.ppermute(
            pick(parts, (col + step) & 3, 0).astype(BF),
            "dp",
            [(d, (d + 4 * step) % 16) for d in range(16)],
        )
        total = total + got.astype(F32)
    return total


def body(tokens, cotangent, first_right, first_left, second_right, second_left):
    count = tokens.shape[0]
    own = first_right.shape[0]
    size = first_right.shape[1]
    groups = size // own
    tok_blocks = tokens.reshape(count, own, size)
    cot_blocks = cotangent.reshape(count, own, size)

    def spread_out(local):
        sent = local.reshape(own, groups, own, count).transpose(1, 0, 2, 3)
        return swap(sent).reshape(size, own, count)

    mixed = jnp.einsum("tij,ijk->ikt", tok_blocks, first_right, preferred_element_type=F32)
    spread = spread_out(mixed.astype(BF))
    grad_local = jnp.einsum("til,ikl->ikt", cot_blocks, second_left, preferred_element_type=F32)
    grad_narrow = spread_out(grad_local.astype(BF))
    pre = jnp.einsum("ikt,kih->kht", spread, first_left, preferred_element_type=F32)
    hidden_act = activate(pre).astype(BF)
    narrowed = jnp.einsum("kht,khi->kit", hidden_act, second_right, preferred_element_type=F32)
    returned = spread_out(narrowed.astype(BF))
    grad_act = jnp.einsum("ikt,khi->kht", grad_narrow, second_right, preferred_element_type=F32)
    grad_pre = activate_grad(pre, grad_act).astype(BF)
    grad_spread = jnp.einsum("kht,kih->kit", grad_pre, first_left, preferred_element_type=F32)
    grad_mixed = spread_out(grad_spread.astype(BF))
    sr_term = jnp.einsum("kht,ikt->hki", hidden_act, grad_narrow, preferred_element_type=F32)
    sr_grad = reduce_dp(sr_term)
    fl_term = jnp.einsum("ikt,kht->ikh", spread, grad_pre, preferred_element_type=F32)
    fl_grad = reduce_dp(fl_term)
    branch_out = jnp.einsum("kit,ikl->til", returned, second_left, preferred_element_type=F32)
    output = (tok_blocks.astype(F32) + branch_out).astype(BF).reshape(count, -1)
    sl_term = jnp.einsum("kit,til->kil", returned, cot_blocks, preferred_element_type=F32)
    sl_grad = reduce_dp(sl_term)
    branch_in = jnp.einsum("kit,ijk->tij", grad_mixed, first_right, preferred_element_type=F32)
    token_grad = (cot_blocks.astype(F32) + branch_in).astype(BF).reshape(count, -1)
    fr_term = jnp.einsum("tij,kit->jik", tok_blocks, grad_mixed, preferred_element_type=F32)
    fr_grad = reduce_dp(fr_term)
    return (output, token_grad, fr_grad, fl_grad, sr_grad, sl_grad)


def solution(mesh):
    placed = (
        P("dp", "feat"),
        P("dp", "feat"),
        P("feat", None, None),
        P("feat", None, None),
        P("feat", None, None),
        P("feat", None, None),
    )
    return jax.shard_map(
        body,
        mesh=mesh,
        in_specs=placed,
        out_specs=(
            P("dp", "feat"),
            P("dp", "feat"),
            P("dp", "feat", None),
            P("dp", "feat", None),
            P("dp", "feat", None),
            P("dp", "feat", None),
        ),
        check_vma=False,
    )
```
